32 devices in a mesh: rows: 8 (over z, x), scales: 4 (over y, core).
Axes of the slice: x: 2, y: 2, z: 4, core: 2. Of those that a mesh axis runs over, the one named last changes fastest.
Arguments:
- image_now: float32 [256, 8192], P(('rows', 'scales')), may hold values from 0.1 to 4
- gradient: float32 [256, 8192], P(('rows', 'scales')), may hold values from -140 to 140
- hessian_weight: float32 [256, 8192], P(('rows', 'scales')), may hold values from 0.1 to 10
- psf_tiles: float32 [32, 256], P(('rows', 'scales')), may hold values from -0.5 to 1.7
- facet_of_row: int32 [256], P(('rows', 'scales')), may hold values from 0 to 31, never falling along the last dimension, each value on 1 to 32 neighbouring positions
- tile_slot: int32 [32], replicated, may hold values from 0 to 31, each once
- thresholds: float32 [4], replicated, may hold values from 0.2 to 2
Outputs:
- new_image: float32 [256, 8192], P(('rows', 'scales'))
The draws below stay inside these ranges and needn't reach their ends.
Inputs may be any that keep to these rules, and one draw needn't show every extreme that they name: `facet_of_row`: facet numbers never fall along the rows; every facet covers 1 to 32 rows, and some facet exactly 32. `tile_slot`: each facet's tile stands in a different row of psf_tiles, and every row holds one.
All inputs are finite; a program needn't handle non-finite values.
Results may differ from the reference program's by a relative error of at most 0.0001.
Values sent between devices are 32-bit elements; how exact they have to be, the bound alone decides.
A program may use at most 64 MiB of HBM per device.

```python
import math
import jax
import jax.numpy as jnp
import numpy as np
from jax import lax

COLS = 8192
TILE = 16
SUBITERS = 2
SCALES = 4
HEIGHT = 256
FACETS = 32
FMOST = 32


def draw_gradient(key, part):
    key_noise, key_rows, key_cols = jax.random.split(key, 3)
    position = jnp.arange(HEIGHT, dtype=jnp.float32)[:, None] / HEIGHT
    rising = jnp.exp(math.log(3.0) * position)
    row_scale = jnp.exp(jax.random.uniform(key_rows, (HEIGHT, 1), minval=0.0, maxval=math.log(10.0))) * rising
    col_scale = jnp.exp(jax.random.uniform(key_cols, (1, COLS), minval=0.0, maxval=math.log(10.0)))
    pattern = jnp.clip(jax.random.normal(key_noise, (HEIGHT, COLS)), -6.0, 6.0)
    return (0.03 * pattern * row_scale * col_scale).astype(jnp.float32)


def draw_hessian_weight(key, part):
    key_cells, key_rows = jax.random.split(key, 2)
    cells = jnp.exp(jax.random.uniform(key_cells, (HEIGHT, COLS), minval=math.log(0.1), maxval=0.0))
    row_scale = jnp.exp(jax.random.uniform(key_rows, (HEIGHT, 1), minval=0.0, maxval=math.log(10.0)))
    return (cells * row_scale).astype(jnp.float32)


def draw_psf_tiles(key, part):
    key_side, key_peak = jax.random.split(key, 2)
    centre = (jnp.arange(TILE * TILE) == TILE // 2 * TILE + TILE // 2)[None, :]
    side_lobes = 0.1 * jnp.clip(jax.random.normal(key_side, (FACETS, TILE * TILE)), -4.0, 4.0)
    peak_value = jax.random.uniform(key_peak, (FACETS, 1), minval=0.8, maxval=1.2)
    return jnp.where(centre, peak_value + side_lobes, side_lobes).astype(jnp.float32)


def level_of(key, shape, cuts, least, largest):
    def one(dim, parts):
        heights = jax.random.uniform(jax.random.fold_in(jax.random.fold_in(key, 6), dim), (parts,), jnp.float32, least / len(cuts), largest / len(cuts))
        return jnp.repeat(jnp.exp(heights), shape[dim] // parts).reshape((-1,) + (1,) * (len(shape) - dim - 1))

    gain = one(*cuts[0])
    for cut in cuts[1:]:
        gain = gain * one(*cut)
    return gain


def profile(number_of, total, reach, slope):
    loads = [(1 << 20) // math.isqrt(grade ** slope) + 1 for grade in range(2, number_of + 1)]
    spare, given = total - reach - (number_of - 1), [1] * (number_of - 1)
    while spare > 0:
        movable = [i for i in range(number_of - 1) if given[i] < reach]
        whole, budget = sum([loads[i] for i in movable]), spare
        for i in movable:
            extra = min(reach - given[i], max(1, budget * loads[i] // whole), spare)
            given[i] = given[i] + extra
            spare = spare - extra
    return np.array([reach] + given)


def ragged_sizes(key, count, total, bound, lean):
    if count == 2:
        one = jax.random.randint(key, (), max(1, total - bound), min(bound, total - 1) + 1)
        return jnp.stack([one, total - one])
    sizes = jnp.asarray(profile(count, total, bound, lean), jnp.int32)
    couples = (count - 1) // 2
    source_of, receiver = sizes[1:1 + 2 * couples:2], sizes[2:2 + 2 * couples:2]
    slack = jnp.minimum(source_of - 1, bound - receiver)
    moved = jax.random.randint(jax.random.fold_in(key, 1), (couples,), 0, 1 << 20) % (slack + 1)
    sizes = sizes.at[1:1 + 2 * couples:2].set(source_of - moved).at[2:2 + 2 * couples:2].set(receiver + moved)
    return sizes[jax.random.permutation(jax.random.fold_in(key, 2), count)]


def setup_inputs(seed: int = 0) -> dict:
    streams_of = jax.random.split(jax.random.key(seed), 8)
    return {
        "image_now": jnp.clip(jnp.exp(math.log(4.0) - 3.6888794 * jax.random.uniform(streams_of[0], (HEIGHT, COLS), jnp.float32) ** level_of(streams_of[0], (HEIGHT, COLS), ((0, 32),), -0.2, 0.2)), 0.1, 4.0),
        "gradient": draw_gradient(jax.random.fold_in(streams_of[7], 71), 0),
        "hessian_weight": draw_hessian_weight(jax.random.fold_in(streams_of[7], 71), 0),
        "psf_tiles": draw_psf_tiles(jax.random.fold_in(streams_of[7], 71), 0),
        "facet_of_row": jnp.searchsorted(jnp.cumsum(ragged_sizes(streams_of[4], FACETS, HEIGHT, FMOST, 2)), jnp.arange(HEIGHT), side="right").astype(jnp.int32),
        "tile_slot": jax.random.permutation(streams_of[5], FACETS).astype(jnp.int32),
        "thresholds": jnp.clip(jnp.exp(jax.random.uniform(streams_of[6], (SCALES,), jnp.float32, math.log(0.2), math.log(2.0))), 0.2, 2.0),
    }


SPLINE_EDGE = 0.0625
SPLINE_NEAR = 0.25
SPLINE_MID = 0.375


def along_columns(source, spacing):
    length = source.shape[1]
    padded = jnp.pad(source, ((0, 0), (2 * spacing, 2 * spacing)))
    outer_pair = padded[:, 0:length] + padded[:, 4 * spacing:4 * spacing + length]
    inner_pair = padded[:, spacing:spacing + length] + padded[:, 3 * spacing:3 * spacing + length]
    return SPLINE_EDGE * outer_pair + SPLINE_NEAR * inner_pair + SPLINE_MID * source


def along_rows(source, spacing):
    length = source.shape[0]
    padded = jnp.pad(source, ((2 * spacing, 2 * spacing), (0, 0)))
    outer_pair = padded[0:length] + padded[4 * spacing:4 * spacing + length]
    inner_pair = padded[spacing:spacing + length] + padded[3 * spacing:3 * spacing + length]
    return SPLINE_EDGE * outer_pair + SPLINE_NEAR * inner_pair + SPLINE_MID * source


def forward_blur(source, weights):
    height, columns = source.shape
    half_tile = TILE // 2
    padded = jnp.pad(source, ((half_tile, half_tile), (half_tile, half_tile)))

    def add_tap_row(tap_row, summed):
        shifted = lax.dynamic_slice_in_dim(padded, tap_row, height, 0)
        tap_weights = lax.dynamic_index_in_dim(weights, tap_row, 1, keepdims=False)
        for column in range(TILE):
            summed = summed + tap_weights[:, column:column + 1] * shifted[:, column:column + columns]
        return summed

    return lax.fori_loop(0, TILE, add_tap_row, jnp.zeros((height, columns), jnp.float32))


def adjoint_blur(source, weights):
    height, columns = source.shape
    half_tile = TILE // 2
    padded = jnp.pad(source, ((half_tile, half_tile), (half_tile, half_tile)))
    wide_weights = jnp.pad(weights, ((half_tile, half_tile), (0, 0), (0, 0)))

    def add_tap_row(tap_row, summed):
        offset = 2 * half_tile - tap_row
        shifted = lax.dynamic_slice_in_dim(padded, offset, height, 0)
        weight_rows = lax.dynamic_slice_in_dim(wide_weights, offset, height, 0)
        tap_weights = lax.dynamic_index_in_dim(weight_rows, tap_row, 1, keepdims=False)
        for column in range(TILE):
            offset_col = 2 * half_tile - column
            summed = summed + tap_weights[:, column:column + 1] * shifted[:, offset_col:offset_col + columns]
        return summed

    return lax.fori_loop(0, TILE, add_tap_row, jnp.zeros((height, columns), jnp.float32))


def shrink(trial, step_size, thresholds):
    smooth = trial
    summed = jnp.zeros_like(trial)
    for depth in range(SCALES):
        smoother = along_rows(along_columns(smooth, 2 ** depth), 2 ** depth)
        detail = smooth - smoother
        limit = step_size * thresholds[depth]
        summed = summed + (detail - jnp.clip(detail, -limit, limit))
        smooth = smoother
    return summed + smooth


def reference(image_now, gradient, hessian_weight, psf_tiles, facet_of_row, tile_slot, thresholds):
    slot_rows = jnp.take(tile_slot, facet_of_row).astype(jnp.int32)
    weights = jnp.take(psf_tiles, slot_rows, axis=0).reshape(HEIGHT, TILE, TILE)
    current = image_now
    for sweep in range(SUBITERS):
        change = current - image_now
        pushed = hessian_weight * forward_blur(change, weights)
        descent = gradient + adjoint_blur(pushed, weights)
        blurred = forward_blur(descent, weights)
        step_size = jnp.sum(descent * descent) / jnp.sum(hessian_weight * blurred * blurred)
        current = shrink(current - step_size * descent, step_size, thresholds)
    return current
```

```python
import functools

import jax
import jax.numpy as jnp
from jax import lax
from jax.experimental import pallas as pl
from jax.experimental.pallas import tpu as pltpu
from jax.sharding import PartitionSpec as P

TILE = 16
HALF = TILE // 2
SUBITERS = 2
LANES = 128
SHIFTS = 4
AXES = ("rows", "scales")
MESH = pl.DeviceIdType.MESH
VMEM = pl.BlockSpec(memory_space=pltpu.VMEM)


def up8(n):
    return -(-n // 8) * 8


def halves(x):
    high = x.astype(jnp.bfloat16)
    low = (x - high.astype(jnp.float32)).astype(jnp.bfloat16)
    return high, low


def dot(a, b):
    return jnp.dot(a, b, preferred_element_type=jnp.float32)


def dot_t(a, b):
    return lax.dot_general(a, b, (((1,), (1,)), ((), ())), preferred_element_type=jnp.float32)


def over(low, high, size, body):
    count = (high - low) // size
    assert count * size == high - low

    def one(n, carry):
        body(pl.multiple_of(low + n * size, 8))
        return carry

    lax.fori_loop(0, count, one, 0)


def block(total, limit, step):
    for size in range(limit // step * step, 0, -step):
        if total % size == 0:
            return size


def kernel(
    count, scales, group, levels, margin,
    image, gradient, weight, psf, facet, slot_of, thresholds,
    out,
    land, psf_all, slots, tg, ti, th, cur, work, smooth, y, sh, sl, cc, sums, pack_up, pack_down, got_up, got_down, back,
    psf_send, psf_recv, slot_send, slot_recv, in_send, in_recv, fwd_send, fwd_recv,
    sum_send, sum_recv, halo_send, halo_recv, out_send, out_recv,
):
    me = lax.axis_index("rows") * scales + lax.axis_index("scales")
    team, place = me // group, me % group
    teams = count // group
    band = image.shape[0]
    columns = image.shape[1]
    own = columns // group
    mid = margin // band
    bands = LANES // band
    side = margin + (SUBITERS - 1) * (margin + TILE)
    off = side + margin
    has_up, has_down = team > 0, team < teams - 1
    first, last = place == 0, place == group - 1
    barrier = pltpu.get_barrier_semaphore()
    lane = lax.broadcasted_iota(jnp.int32, (1, LANES), 1)

    def device(index):
        return (index // scales, index % scales)

    def peer(k):
        return (me + k) % count

    def greet(k, carry):
        pl.semaphore_signal(barrier, inc=1, device_id=device(peer(k)), device_id_type=MESH)
        return carry

    lax.fori_loop(1, count, greet, 0)

    def copy(src, dst, send_sem, recv_sem, index):
        return pltpu.make_async_remote_copy(
            src_ref=src, dst_ref=dst, send_sem=send_sem, recv_sem=recv_sem,
            device_id=device(index), device_id_type=MESH,
        )

    def share(src, pool, send, recv):
        def start(k, carry):
            copy(src, pool.at[me], send.at[k], recv.at[me], peer(k)).start()
            return carry

        lax.fori_loop(1, count, start, 0)

    def collect(src, pool, send, recv):
        def wait(k, carry):
            copy(src, pool.at[peer(k)], send.at[k], recv.at[peer(k)], peer(k)).wait()
            return carry

        lax.fori_loop(1, count, wait, 0)

    def piece(e, j):
        src = (image, gradient, weight)[e]
        low, high = max(j * own - LANES, 0), min((j + 1) * own + LANES, columns)
        start = low - (j * own - LANES)
        return src.at[:, low:high], land.at[e, mid + place, :, start : start + high - low]

    def in_start(e):
        for j in range(group):
            src, dst = piece(e, j)

            @pl.when(place != j)
            def _():
                copy(src, dst, in_send.at[e, j], in_recv.at[e, place], team * group + j).start()

            @pl.when(place == j)
            def _():
                pltpu.make_async_copy(src, dst, in_recv.at[e, j]).start()

    def in_wait(e, k):
        for j, when in ((0, first), (group - 1, last), (1, jnp.logical_not(first | last))):
            low, high = max(j * own - LANES, 0), min((j + 1) * own + LANES, columns)
            start = low - (j * own - LANES)
            dst = land.at[e, mid + k, :, start : start + high - low]

            @pl.when(when)
            def _():
                copy(dst, dst, in_send.at[e, 0], in_recv.at[e, k], me).wait_recv()

    def in_done(e):
        for j in range(group):
            src, dst = piece(e, j)

            @pl.when(place != j)
            def _():
                copy(src, dst, in_send.at[e, j], in_recv.at[e, place], team * group + j).wait_send()

    def forward(e, k, reach):
        out_ = []
        if k < reach:
            out_.append((has_up, me - group, mid + group + k, mid - 1 - k))
        if k >= group - reach:
            out_.append((has_down, me + group, mid - group + k, mid + 2 * group - 1 - k))
        return out_

    def forward_start(e, k, reach):
        for when, index, there, _ in forward(e, k, reach):

            @pl.when(when)
            def _():
                copy(land.at[e, mid + k], land.at[e, there], fwd_send.at[e, there], fwd_recv.at[e, there], index).start()

    def forward_done(e, reach):
        for k in range(group):
            for when, index, there, _ in forward(e, k, reach):

                @pl.when(when)
                def _():
                    copy(land.at[e, mid + k], land.at[e, there], fwd_send.at[e, there], fwd_recv.at[e, there], index).wait_send()

        for r in range(reach):
            for when, here in ((has_up, mid - 1 - r), (has_down, mid + group + r)):

                @pl.when(when)
                def _():
                    copy(land.at[e, here], land.at[e, here], fwd_send.at[e, here], fwd_recv.at[e, here], me).wait_recv()

    def gather_in(e, reach):
        for k in range(group):
            in_wait(e, k)
            forward_start(e, k, reach)

    def turn(e, dst):
        tiles = land.shape[3] // LANES
        for t in range(tiles):
            x = land[e, :, :, t * LANES : (t + 1) * LANES].reshape(LANES, LANES).T
            low = off + (t - 1) * LANES
            cut = max(0, off - side - low)
            stop = min(LANES, off + own + side - low)
            dst[low + cut : low + stop, :] = x[cut:stop, :]

    def clear_sides(ref):
        @pl.when(first)
        def _():
            ref[off - side : off, :] = jnp.zeros((side, LANES), jnp.float32)

        @pl.when(last)
        def _():
            ref[off + own : off + own + side, :] = jnp.zeros((side, LANES), jnp.float32)

    reach_of = (mid, mid, TILE // band)

    @pl.when(first)
    def _():
        land[:, mid : mid + group, :, 0:LANES] = jnp.zeros((3, group, band, LANES), jnp.float32)

    @pl.when(last)
    def _():
        land[:, mid : mid + group, :, own + LANES :] = jnp.zeros((3, group, band, LANES), jnp.float32)

    @pl.when(jnp.logical_not(has_up))
    def _():
        land[:, 0:mid] = jnp.zeros((3, mid) + land.shape[2:], jnp.float32)
        slots[0:mid] = jnp.full((mid, band, LANES), -1.0, jnp.float32)
        got_up[...] = jnp.zeros_like(got_up)

    @pl.when(jnp.logical_not(has_down))
    def _():
        land[:, mid + group :] = jnp.zeros((3, mid) + land.shape[2:], jnp.float32)
        slots[mid + group :] = jnp.full((mid, band, LANES), -1.0, jnp.float32)
        got_down[...] = jnp.zeros_like(got_down)

    spare = mid - reach_of[2]
    for low in (0, bands - spare):
        land[2, low : low + spare] = jnp.zeros((spare,) + land.shape[2:], jnp.float32)
        slots[low : low + spare] = jnp.full((spare, band, LANES), -1.0, jnp.float32)

    sub = lax.broadcasted_iota(jnp.int32, (band, LANES), 0)
    mine = jnp.zeros((band, LANES), jnp.int32)
    for r in range(band):
        mine = jnp.where(sub == r, slot_of[facet[r]], mine)
    slots[mid + place] = mine.astype(jnp.float32)

    inside = jnp.where(has_up, 1, lane >= margin) * jnp.where(has_down, 1, lane < LANES - margin)
    inside = inside.astype(jnp.float32)
    for k in range(levels):
        d = 2**k
        i = lax.broadcasted_iota(jnp.int32, (2 * LANES, LANES), 0) % LANES
        o = jnp.abs(i - lax.broadcasted_iota(jnp.int32, (2 * LANES, LANES), 1))
        coef = jnp.where(o == 0, 0.375, jnp.where(o == d, 0.25, jnp.where(o == 2 * d, 0.0625, 0.0)))
        cc[k] = (coef * inside).astype(jnp.bfloat16)

    pl.semaphore_wait(barrier, count - 1)

    slot_src = slots.at[mid + place]
    near = reach_of[2]

    def slot_to(fn):
        for j in range(group):

            @pl.when(place != j)
            def _():
                fn(slot_src, slots.at[mid + place], slot_send.at[1, j], slot_recv.at[mid + place], team * group + j)

            @pl.when(has_up & (place < near))
            def _():
                there = mid + group + place
                fn(slot_src, slots.at[there], slot_send.at[0, j], slot_recv.at[there], (team - 1) * group + j)

            @pl.when(has_down & (place >= group - near))
            def _():
                there = mid - group + place
                fn(slot_src, slots.at[there], slot_send.at[2, j], slot_recv.at[there], (team + 1) * group + j)

    slot_to(lambda *a: copy(*a).start())
    share(psf, psf_all, psf_send, psf_recv)
    in_start(1)
    in_start(2)
    in_start(0)
    psf_all[me] = psf[...]
    gather_in(1, reach_of[1])
    collect(psf, psf_all, psf_send, psf_recv)
    slot_to(lambda *a: copy(*a).wait_send())
    for b in range(mid - near, mid + group + near):
        other = has_up if b < mid else has_down if b >= mid + group else place != b - mid

        @pl.when(other)
        def _():
            copy(slots.at[b], slots.at[b], slot_send.at[1, 0], slot_recv.at[b], me).wait_recv()

    rows_slot = slots[...].reshape(LANES, LANES)

    def pick(s, acc):
        tile = psf_all[s]
        hit = rows_slot == s.astype(jnp.float32)
        return tuple(jnp.where(hit, tile[:, h * LANES : (h + 1) * LANES], acc[h]) for h in range(2))

    zero = jnp.zeros((LANES, LANES), jnp.float32)
    taps = jnp.concatenate(lax.fori_loop(0, count, pick, (zero, zero)), axis=1)
    i = lax.broadcasted_iota(jnp.int32, (TILE * TILE, TILE * TILE), 0)
    j = lax.broadcasted_iota(jnp.int32, (TILE * TILE, TILE * TILE), 1)
    swap = ((i // TILE == j % TILE) & (i % TILE == j // TILE)).astype(jnp.float32).astype(jnp.bfloat16)
    high, low = halves(taps)
    taps = dot(high, swap) + dot(low, swap)
    i = lax.broadcasted_iota(jnp.int32, (LANES, LANES), 0)
    j = lax.broadcasted_iota(jnp.int32, (LANES, LANES), 1)
    tap = j - i + HALF
    banded = (tap >= 0) & (tap < TILE)
    per = LANES // TILE
    for h in range(TILE // per):
        skew = pltpu.roll(taps[:, h * LANES : (h + 1) * LANES], LANES - HALF, 1, stride=1, stride_axis=0)
        for n in range(per):
            b = h * per + n
            x = jnp.where(banded, pltpu.roll(skew, LANES - TILE * n, 1) if n else skew, 0.0)
            high, low = halves(x)
            rows = slice(b // SHIFTS * LANES, (b // SHIFTS + 1) * LANES)
            cols = slice(b % SHIFTS * LANES, (b % SHIFTS + 1) * LANES)
            sh[rows, cols] = high
            sl[rows, cols] = low

    forward_done(1, reach_of[1])
    turn(1, tg)

    def multiply(src, low, high, step, table):
        size = block(high - low, 320, 16)

        def one(start):
            x = jnp.concatenate([src[pl.ds(start + low + off + step * n, size), :] for n in range(SHIFTS)], axis=1)
            a, b = halves(x)
            total = table(a, sh[...]) + table(b, sh[...]) + table(a, sl[...])
            for n in range(SHIFTS):
                y[n, pl.ds(start, size), :] = total[:, n * LANES : (n + 1) * LANES]

        over(0, high - low, size, one)

    def added(start, size, shifts):
        total = None
        for n in range(SHIFTS):
            part = y[n, pl.ds(start + shifts[n], size), :]
            total = part if total is None else total + part
        return total

    def blurred(src, low, high, body):
        multiply(src, low - HALF, high + HALF, 1, dot_t)
        size = block(high - low, 256, 8)
        over(low, high, size, lambda c: body(c, size, added(c - low, size, [SHIFTS * n for n in range(SHIFTS)])))

    def adjoint(src, low, high, body):
        multiply(src, low, high + TILE, -SHIFTS, dot)
        size = block(high - low, 256, 8)
        over(low, high, size, lambda c: body(c, size, added(c - low, size, [HALF - n for n in range(SHIFTS)])))

    def step_of(sweep, descent, between):
        back[0:2, :, 0:LANES] = jnp.zeros((2, band, LANES), jnp.float32)

        def tally(c, size, b):
            d = descent[pl.ds(c + off, size), :]
            w = th[pl.ds(c + off, size), :]
            one = (d * d).reshape(size // 8, 8, LANES).sum(axis=0)
            two = (w * b * b).reshape(size // 8, 8, LANES).sum(axis=0)
            back[0, :, 0:LANES] += one
            back[1, :, 0:LANES] += two

        blurred(descent, 0, own, tally)
        keep_rows = (lane >= margin) & (lane < LANES - margin)

        def total(x):
            return jnp.where(keep_rows, jnp.sum(x, axis=0, keepdims=True), 0.0)

        sums[sweep, me] = jnp.concatenate([total(back[0, :, 0:LANES]), total(back[1, :, 0:LANES])], axis=0)
        mine = sums.at[sweep, me]
        share(mine, sums.at[sweep], sum_send.at[sweep], sum_recv.at[sweep])
        between()
        collect(mine, sums.at[sweep], sum_send.at[sweep], sum_recv.at[sweep])
        totals = jnp.sum(jnp.sum(sums[sweep], axis=0), axis=1, keepdims=True)
        return totals[0:1] / totals[1:2]

    def starlet(step, reach, inner, store):
        low, high = off - reach, off + own + reach
        size = block(high - low, 320, 8)
        for k in range(levels):
            d = 2**k
            src, dst = smooth.at[k], smooth.at[k + 1]

            def one(s):
                def at(n):
                    return src[pl.ds(s + n, size), :]

                x = 0.0625 * (at(-2 * d) + at(2 * d)) + 0.25 * (at(-d) + at(d)) + 0.375 * at(0)
                dst[pl.ds(s, size), :] = dot(jnp.concatenate(halves(x), axis=1), cc[k])

            over(low, high, size, one)
            clear_sides(dst)
        limits = [step * thresholds[k] for k in range(levels)]
        low, high = off - inner, off + own + inner
        size = block(high - low, 256, 8)

        def last_pass(s):
            before = smooth[0, pl.ds(s, size), :]
            total = None
            for k in range(levels):
                after = smooth[k + 1, pl.ds(s, size), :]
                detail = before - after
                part = detail - jnp.clip(detail, -limits[k], limits[k])
                total = part if total is None else total + part
                before = after
            store(s, size, total + before)

        over(low, high, size, last_pass)

    def halo_args(n, size):
        return (
            (has_up, pack_up.at[0:size], got_down.at[n, 0:size], halo_send.at[n, 0], halo_recv.at[n, 1], me - group),
            (has_down, pack_down.at[0:size], got_up.at[n, 0:size], halo_send.at[n, 1], halo_recv.at[n, 0], me + group),
        )

    def halo_start(n, ref, inner):
        size = (own + 2 * inner) // (LANES // margin)
        for k in range(LANES // margin):
            x = ref[off - inner + k * size : off - inner + (k + 1) * size, :]
            here = (lane >= k * margin) & (lane < (k + 1) * margin)
            for pack, source in ((pack_up, margin), (pack_down, LANES - 2 * margin)):
                moved = pltpu.roll(x, (k * margin - source) % LANES, 1)
                pack[0:size, :] = moved if k == 0 else jnp.where(here, moved, pack[0:size, :])
        for when, src, dst, send, recv, index in halo_args(n, size):

            @pl.when(when)
            def _():
                copy(src, dst, send, recv, index).start()

    def halo_done(n, inner):
        size = (own + 2 * inner) // (LANES // margin)
        for (when, src, dst, send, recv, index), got, r in zip(halo_args(n, size), (got_up, got_down), (0, 1)):

            @pl.when(when)
            def _():
                copy(src, dst, send, recv, index).wait_send()
                here = got.at[n, 0:size]
                copy(here, here, send, halo_recv.at[n, r], index).wait_recv()

    def with_halo(n, ref, inner):
        size = (own + 2 * inner) // (LANES // margin)
        for k in range(LANES // margin):
            rows = slice(off - inner + k * size, off - inner + (k + 1) * size)
            above = pltpu.roll(got_up[n, 0:size, :], (-k * margin) % LANES, 1)
            below = pltpu.roll(got_down[n, 0:size, :], (LANES - margin - k * margin) % LANES, 1)
            x = jnp.where(lane < margin, above, jnp.where(lane >= LANES - margin, below, ref[rows, :]))
            ref[rows, :] = x

    gather_in(2, reach_of[2])
    forward_done(2, reach_of[2])
    turn(2, th)

    def fetch_image():
        gather_in(0, reach_of[0])
        forward_done(0, reach_of[0])
        turn(0, ti)

    step = step_of(0, tg, fetch_image)

    def trial(step, start, descent, reach):
        low, high = off - reach, off + own + reach

        def one(s):
            smooth[0, pl.ds(s, block(high - low, 256, 8)), :] = (
                start[pl.ds(s, block(high - low, 256, 8)), :] - step * descent[pl.ds(s, block(high - low, 256, 8)), :]
            )

        over(low, high, block(high - low, 256, 8), one)

    trial(step, ti, tg, side)
    inner = margin + TILE

    def store_current(s, size, x):
        cur[pl.ds(s, size), :] = x

    starlet(step, side, inner, store_current)

    halo_start(0, cur, inner)
    halo_done(0, inner)
    with_halo(0, cur, inner)

    def change(s):
        size = block(own + 2 * inner, 256, 8)
        work[pl.ds(s, size), :] = cur[pl.ds(s, size), :] - ti[pl.ds(s, size), :]

    over(off - inner, off + own + inner, block(own + 2 * inner, 256, 8), change)

    def push(c, size, b):
        smooth[0, pl.ds(c + off, size), :] = th[pl.ds(c + off, size), :] * b

    blurred(work, -inner + HALF, own + inner - HALF, push)

    def descend(c, size, b):
        work[pl.ds(c + off, size), :] = (tg[pl.ds(c + off, size), :] + b) * inside

    adjoint(smooth.at[0], -margin, own + margin, descend)
    clear_sides(work)
    halo_start(1, work, margin)
    step = step_of(1, work, lambda: halo_done(1, margin))
    with_halo(1, work, margin)
    trial(step, cur, work, margin)

    def store_back(s, size, x):
        cur[pl.ds(s, size), :] = x

    starlet(step, margin, 0, store_back)
    for t in range(own // LANES):
        x = cur[off + t * LANES : off + (t + 1) * LANES, :].T
        back[:, :, t * LANES : (t + 1) * LANES] = x[margin : LANES - margin].reshape(group, band, LANES)

    def slab(p):
        return out.at[:, pl.ds(pl.multiple_of(p * own, LANES), own)]

    for j in range(group):

        @pl.when(place != j)
        def _():
            copy(back.at[j], slab(place), out_send.at[j], out_recv.at[place], team * group + j).start()

        @pl.when(place == j)
        def _():
            pltpu.make_async_copy(back.at[j], slab(place), out_recv.at[j]).start()

    for e in range(3):
        in_done(e)
    for j in range(group):

        @pl.when(place != j)
        def _():
            copy(back.at[j], slab(place), out_send.at[j], out_recv.at[place], team * group + j).wait_send()

        copy(back.at[j], slab(j), out_send.at[j], out_recv.at[j], me).wait_recv()


def body(image_now, gradient, hessian_weight, psf_tiles, facet_of_row, tile_slot, thresholds):
    band, columns = image_now.shape
    levels = thresholds.shape[0]
    scales = lax.axis_size("scales")
    count = lax.axis_size("rows") * scales
    margin = up8(2 ** (levels + 1) - 2)
    group = (LANES - 2 * margin) // band
    own = columns // group
    teams = count // group
    side = margin + (SUBITERS - 1) * (margin + TILE)
    rows = own + 2 * side + 2 * margin
    bands = LANES // band
    f32 = lambda *shape: pltpu.VMEM(shape, jnp.float32)
    bf16 = lambda *shape: pltpu.VMEM(shape, jnp.bfloat16)
    sem = lambda *shape: pltpu.SemaphoreType.DMA(shape)
    smem = pl.BlockSpec(memory_space=pltpu.SMEM)
    plane = (rows, LANES)
    wide = SHIFTS * LANES
    halo = (own + 2 * (margin + TILE)) // (LANES // margin)
    return pl.pallas_call(
        functools.partial(kernel, count, scales, group, levels, margin),
        out_shape=jax.ShapeDtypeStruct((band, columns), jnp.float32),
        in_specs=[VMEM] * 4 + [smem] * 3,
        out_specs=VMEM,
        scratch_shapes=[
            f32(3, bands, band, own + 2 * LANES), f32(count, 1, TILE * TILE), f32(bands, band, LANES),
            f32(*plane), f32(*plane), f32(*plane), f32(*plane), f32(*plane), f32(levels + 1, *plane),
            f32(SHIFTS, *plane), bf16(wide, wide), bf16(wide, wide), bf16(levels, 2 * LANES, LANES),
            f32(SUBITERS, count, 2, LANES), f32(halo, LANES), f32(halo, LANES), f32(SUBITERS, halo, LANES),
            f32(SUBITERS, halo, LANES), f32(group, band, own),
            sem(count), sem(count), sem(3, group), sem(bands), sem(3, group), sem(3, group),
            sem(3, bands), sem(3, bands), sem(SUBITERS, count), sem(SUBITERS, count),
            sem(SUBITERS, 2), sem(SUBITERS, 2), sem(group), sem(group),
        ],
        compiler_params=pltpu.CompilerParams(
            collective_id=0, has_side_effects=True, vmem_limit_bytes=56 * 1024 * 1024
        ),
    )(image_now, gradient, hessian_weight, psf_tiles, facet_of_row, tile_slot, thresholds)


def solution(mesh):
    band = P(AXES, None)
    in_specs = (band, band, band, band, P(AXES), P(), P())
    return jax.shard_map(body, mesh=mesh, in_specs=in_specs, out_specs=band, check_vma=False)
```
